32 devices in a mesh: gx: 8 (over z, x), gy: 4 (over y, core).
Axes of the slice: x: 2, y: 2, z: 4, core: 2. Of those that a mesh axis runs over, the one named last changes fastest.
Arguments:
- maps: bfloat16 [8, 4, 2048, 2048], P('gx', 'gy'), may hold values from -0.125 to 0.125
- sources: float32 [8, 4, 256, 2048], P('gx', 'gy'), may hold values from -6 to 6
- traces: bfloat16 [8, 4, 256, 2048], P('gx', 'gy'), may hold values from -6 to 6
Outputs:
- outgoing: bfloat16 [8, 4, 256, 2048], P('gx', 'gy')
The draws below stay inside these ranges and needn't reach their ends.
All inputs are finite; a program needn't handle non-finite values.
Results may differ from the reference program's by a relative error of at most 0.0085.
Values may be sent and summed in bfloat16 or wider, within the bound.
A program may use at most 64 MiB of HBM per device.

```python
import jax
import jax.numpy as jnp
from jax import lax

FACE = 512
MAPN = 2048
RHS = 256
TICKS = 8
PX = 8
PY = 4


def steps_of(stream_key, shape, cuts, least, top_value):
    gain = 1.0
    for dim, parts in cuts:
        draws = jax.random.uniform(jax.random.fold_in(jax.random.fold_in(stream_key, 6), dim), (parts,), jnp.float32, least / len(cuts), top_value / len(cuts))
        gain = gain * jnp.repeat(jnp.exp(draws), shape[dim] // parts).reshape((-1,) + (1,) * (len(shape) - 1 - dim))
    return gain


def scatter_about(own_key, shape, spread, bound, split=(), held_as=jnp.bfloat16):
    values = jax.random.normal(own_key, shape, jnp.float32) * spread
    if len(split) > 0:
        values = steps_of(own_key, shape, split, -0.22, 0.18) * values
    return jnp.clip(values, min=-bound, max=bound).astype(held_as)


def setup_inputs(seed: int = 0) -> dict:
    splits = jax.random.split(jax.random.key(seed), 4)
    return {
        "maps": scatter_about(splits[0], (PX, PY, MAPN, MAPN), MAPN ** -0.5, 0.125, ((0, 8), (1, 4))),
        "sources": scatter_about(splits[1], (PX, PY, RHS, MAPN), 1.0, 6.0, ((0, 8), (1, 4)), jnp.float32),
        "traces": scatter_about(splits[2], (PX, PY, RHS, MAPN), 1.0, 6.0, ((0, 8), (1, 4))),
    }


def products(state, maps, sources, low, width):
    def one(items):
        block, matrix, source = items
        value = jnp.dot(block, matrix[:, low:low + width], preferred_element_type=jnp.float32)
        return (value + source[:, low:low + width]).astype(jnp.bfloat16)

    def flat(array):
        return array.reshape((PX * PY,) + array.shape[2:])

    result = lax.map(one, (flat(state), flat(maps), flat(sources)))
    return result.reshape((PX, PY) + result.shape[1:])


def reference(maps, sources, traces):
    face = FACE
    state = traces
    for tick in range(TICKS):
        if tick == TICKS - 1:
            return products(state, maps, sources, 0, 4 * face)
        if tick < TICKS // 2:
            faces = products(state, maps, sources, 2 * face, 2 * face)
            east = faces[..., :face]
            north = faces[..., face:]
            west_new = jnp.concatenate([jnp.zeros_like(east[:1]), east[:-1]], axis=0)
            south_new = jnp.concatenate([jnp.zeros_like(north[:, :1]), north[:, :-1]], axis=1)
            state = jnp.concatenate([west_new, south_new, state[..., 2 * face:]], axis=-1)
        else:
            faces = products(state, maps, sources, 0, 2 * face)
            west = faces[..., :face]
            south = faces[..., face:]
            east_new = jnp.concatenate([west[1:], jnp.zeros_like(west[:1])], axis=0)
            north_new = jnp.concatenate([south[:, 1:], jnp.zeros_like(south[:, :1])], axis=1)
            state = jnp.concatenate([state[..., :2 * face], east_new, north_new], axis=-1)
    return state
```

```python
import functools

import jax
import jax.numpy as jnp
from jax import lax
from jax.experimental import pallas as pl
from jax.experimental.pallas import tpu as pltpu
from jax.sharding import PartitionSpec as P

TICKS = 8
CHUNKS = 4
MESH = pl.DeviceIdType.MESH


def dot(a, b):
    return jnp.dot(a, b, preferred_element_type=jnp.float32)


def sweep(
    maps_hbm, sources_hbm, traces_hbm, out_hbm,
    maps, sources, traces, held_down, held_up, held_last, first_up, result,
    send_x, send_y, recv_x, recv_y,
    maps_sem, sources_sem, traces_sem, out_sem, ssx, ssy, rsx, rsy,
):
    face = traces.shape[-1] // 4
    rows = traces.shape[1]
    last = TICKS - 1
    turn = TICKS // 2
    low, high = slice(0, 2 * face), slice(2 * face, 4 * face)
    i, j = lax.axis_index("gx"), lax.axis_index("gy")
    px, py = lax.axis_size("gx"), lax.axis_size("gy")
    has_left, has_right = i > 0, i < px - 1
    has_below, has_above = j > 0, j < py - 1

    def load_maps(row, col, col_faces, sem):
        window = (pl.ds(row * face, 2 * face), pl.ds(col * face, col_faces * face))
        return pltpu.make_async_copy(maps_hbm.at[(0, 0) + window], maps.at[window], maps_sem.at[sem])

    def load_sources(col, col_faces, sem):
        columns = pl.ds(col * face, col_faces * face)
        return [
            pltpu.make_async_copy(
                sources_hbm.at[0, 0, pl.ds(c * rows, rows), columns], sources.at[c, :, columns], sources_sem.at[sem, c]
            )
            for c in range(CHUNKS)
        ]

    load_traces = [
        pltpu.make_async_copy(traces_hbm.at[0, 0, pl.ds(c * rows, rows)], traces.at[c], traces_sem.at[c])
        for c in range(CHUNKS)
    ]
    east_sources, north_sources, low_sources = load_sources(2, 1, 0), load_sources(3, 1, 1), load_sources(0, 2, 2)
    high_east, low_east = load_maps(2, 2, 1, 0), load_maps(0, 2, 1, 1)
    high_north, low_north = load_maps(2, 3, 1, 2), load_maps(0, 3, 1, 3)
    high_low, low_low = load_maps(2, 0, 2, 4), load_maps(0, 0, 2, 5)
    for copy in load_traces + [high_east] + east_sources + [low_east, high_north] + north_sources + [low_north]:
        copy.start()
    for copy in [high_low] + low_sources + [low_low]:
        copy.start()

    barrier = pltpu.get_barrier_semaphore()
    neighbours = ((has_left, "gx", i - 1), (has_right, "gx", i + 1), (has_below, "gy", j - 1), (has_above, "gy", j + 1))
    for there, axis, index in neighbours:
        @pl.when(there)
        def _():
            pl.semaphore_signal(barrier, inc=1, device_id={axis: index}, device_id_type=MESH)
    pl.semaphore_wait(barrier, sum(there.astype(jnp.int32) for there, _, _ in neighbours))

    def copy_x(t, c, target):
        return pltpu.make_async_remote_copy(
            src_ref=send_x.at[t, c], dst_ref=recv_x.at[t, c], send_sem=ssx.at[t, c], recv_sem=rsx.at[t, c],
            device_id={"gx": target}, device_id_type=MESH,
        )

    def copy_y(t, c, target):
        return pltpu.make_async_remote_copy(
            src_ref=send_y.at[t, c], dst_ref=recv_y.at[t, c], send_sem=ssy.at[t, c], recv_sem=rsy.at[t, c],
            device_id={"gy": target}, device_id_type=MESH,
        )

    def put(copy, there, buffer, t, c, value, target):
        buffer[t, c] = value.astype(buffer.dtype)

        @pl.when(there)
        def _():
            copy(t, c, target).start()

    put_east = functools.partial(put, copy_x, has_right, send_x, target=i + 1)
    put_north = functools.partial(put, copy_y, has_above, send_y, target=j + 1)
    put_west = functools.partial(put, copy_x, has_left, send_x, target=i - 1)
    put_south = functools.partial(put, copy_y, has_below, send_y, target=j - 1)

    def await_faces(t, c, there_x, there_y):
        @pl.when(there_y)
        def _():
            copy_y(t, c, j).wait_recv()

        @pl.when(there_x)
        def _():
            copy_x(t, c, i).wait_recv()

    def clear(buffer, there, begin, end):
        @pl.when(jnp.logical_not(there))
        def _():
            buffer[begin:end] = jnp.zeros((end - begin,) + buffer.shape[1:], buffer.dtype)

    def cols(k):
        return slice(k * face, (k + 1) * face)

    for k, put_face, high_copy, low_copy, source_copies in (
        (2, put_east, high_east, low_east, east_sources),
        (3, put_north, high_north, low_north, north_sources),
    ):
        if k == 2:
            for copy in load_traces:
                copy.wait()
        high_copy.wait()
        low_copy.wait()
        for copy in source_copies:
            copy.wait()

        def first(c, carry):
            held_down[c, :, cols(k - 2)] = dot(traces[c, :, high], maps[high, cols(k)]) + sources[c, :, cols(k)]
            put_face(0, c, dot(traces[c, :, low], maps[low, cols(k)]) + held_down[c, :, cols(k - 2)])
            return carry

        lax.fori_loop(0, CHUNKS, first, 0)

    clear(recv_x, has_left, 0, turn)
    clear(recv_y, has_below, 0, turn)
    clear(recv_x, has_right, turn, last)
    clear(recv_y, has_above, turn, last)

    high_low.wait()
    low_low.wait()
    for copy in low_sources:
        copy.wait()

    def ahead(c, carry):
        first_up[c] = dot(traces[c, :, high], maps[high, low]) + sources[c, :, low]
        return carry

    def arrived(t, c, row, columns):
        x = dot(recv_x[t, c], maps[row * face : (row + 1) * face, columns])
        y = dot(recv_y[t, c], maps[(row + 1) * face : (row + 2) * face, columns])
        return x + y

    def down(step, carry):
        t, c = step // CHUNKS + 1, step % CHUNKS
        await_faces(t - 1, c, has_left, has_below)
        put_east(t, c, arrived(t - 1, c, 0, cols(2)) + held_down[c, :, cols(0)])
        put_north(t, c, arrived(t - 1, c, 0, cols(3)) + held_down[c, :, cols(1)])
        return carry

    lax.fori_loop(0, CHUNKS, down, 0)
    lax.fori_loop(0, CHUNKS, ahead, 0)
    lax.fori_loop(CHUNKS, (turn - 1) * CHUNKS, down, 0)

    def turned(c, carry):
        await_faces(turn - 1, c, has_left, has_below)
        for k, put_face in ((0, put_west), (1, put_south)):
            value = arrived(turn - 1, c, 0, cols(k))
            put_face(turn, c, value + first_up[c, :, cols(k)])
            held_up[c, :, cols(k)] = value + sources[c, :, cols(k)]
        return carry

    lax.fori_loop(0, CHUNKS, turned, 0)

    def late(c, carry):
        held_last[c] = arrived(turn - 1, c, 0, high) + sources[c, :, high]
        return carry

    def up(step, carry):
        t, c = step // CHUNKS + turn + 1, step % CHUNKS
        await_faces(t - 1, c, has_right, has_above)
        put_west(t, c, arrived(t - 1, c, 2, cols(0)) + held_up[c, :, cols(0)])
        put_south(t, c, arrived(t - 1, c, 2, cols(1)) + held_up[c, :, cols(1)])
        return carry

    lax.fori_loop(0, CHUNKS, up, 0)
    lax.fori_loop(0, CHUNKS, late, 0)
    lax.fori_loop(CHUNKS, (last - turn - 1) * CHUNKS, up, 0)

    def store_out(c):
        return pltpu.make_async_copy(result.at[c], out_hbm.at[0, 0, pl.ds(c * rows, rows)], out_sem.at[c])

    for c in range(CHUNKS):
        await_faces(last - 1, c, has_right, has_above)
        result[c, :, low] = (arrived(last - 1, c, 2, low) + held_up[c]).astype(result.dtype)
        result[c, :, high] = (arrived(last - 1, c, 2, high) + held_last[c]).astype(result.dtype)
        store_out(c).start()

    def sent(begin, end, there_x, there_y):
        def one(step, carry):
            t, c = step // CHUNKS + begin, step % CHUNKS

            @pl.when(there_x)
            def _():
                copy_x(t, c, i).wait_send()

            @pl.when(there_y)
            def _():
                copy_y(t, c, j).wait_send()

            return carry

        lax.fori_loop(0, (end - begin) * CHUNKS, one, 0)

    sent(0, turn, has_right, has_above)
    sent(turn, last, has_left, has_below)
    for c in range(CHUNKS):
        store_out(c).wait()


def on_device(maps, sources, traces):
    total, width = traces.shape[2:]
    face = width // 4
    rows = total // CHUNKS
    swaps = TICKS - 1

    def faces():
        return pltpu.VMEM((swaps, CHUNKS, rows, face), jnp.bfloat16)

    def wide(columns, dtype):
        return pltpu.VMEM((CHUNKS, rows, columns), dtype)

    dma = pltpu.SemaphoreType.DMA
    return pl.pallas_call(
        sweep,
        out_shape=jax.ShapeDtypeStruct(traces.shape, jnp.bfloat16),
        in_specs=[pl.BlockSpec(memory_space=pl.ANY)] * 3,
        out_specs=pl.BlockSpec(memory_space=pl.ANY),
        scratch_shapes=[
            pltpu.VMEM((width, width), jnp.bfloat16),
            wide(width, jnp.float32),
            wide(width, jnp.bfloat16),
            wide(2 * face, jnp.float32),
            wide(2 * face, jnp.float32),
            wide(2 * face, jnp.float32),
            wide(2 * face, jnp.float32),
            wide(width, jnp.bfloat16),
            faces(),
            faces(),
            faces(),
            faces(),
            dma((6,)),
            dma((3, CHUNKS)),
            dma((CHUNKS,)),
            dma((CHUNKS,)),
        ]
        + [dma((swaps, CHUNKS))] * 4,
        compiler_params=pltpu.CompilerParams(collective_id=0, has_side_effects=True),
    )(maps, sources, traces)


def solution(mesh):
    spec = P("gx", "gy", None, None)
    return jax.shard_map(on_device, mesh=mesh, in_specs=(spec, spec, spec), out_specs=spec, check_vma=False)
```

```python
import functools

import jax
import jax.numpy as jnp
from jax import lax
from jax.experimental import pallas as pl
from jax.experimental.pallas import tpu as pltpu
from jax.sharding import PartitionSpec as P

TICKS = 8
CHUNKS = 2
MESH = pl.DeviceIdType.MESH


def dot(a, b):
    return jnp.dot(a, b, preferred_element_type=jnp.float32)


def sweep(
    maps_hbm, sources_hbm, traces_hbm, out_hbm,
    maps, sources, traces, held_down, held_up, held_last, first_up, partial, result,
    send_x, send_y, recv_x, recv_y,
    maps_sem, sources_sem, traces_sem, out_sem, ssx, ssy, rsx, rsy,
):
    face = traces.shape[-1] // 4
    rows = traces.shape[1]
    last = TICKS - 1
    turn = TICKS // 2
    low, high = slice(0, 2 * face), slice(2 * face, 4 * face)
    i, j = lax.axis_index("gx"), lax.axis_index("gy")
    px, py = lax.axis_size("gx"), lax.axis_size("gy")
    has_left, has_right = i > 0, i < px - 1
    has_below, has_above = j > 0, j < py - 1

    def load_maps(row, col, col_faces, sem):
        window = (pl.ds(row * face, 2 * face), pl.ds(col * face, col_faces * face))
        return pltpu.make_async_copy(maps_hbm.at[(0, 0) + window], maps.at[window], maps_sem.at[sem])

    def load_sources(col, col_faces, sem):
        columns = pl.ds(col * face, col_faces * face)
        return [
            pltpu.make_async_copy(
                sources_hbm.at[0, 0, pl.ds(c * rows, rows), columns], sources.at[c, :, columns], sources_sem.at[sem, c]
            )
            for c in range(CHUNKS)
        ]

    load_traces = [
        pltpu.make_async_copy(traces_hbm.at[0, 0, pl.ds(c * rows, rows)], traces.at[c], traces_sem.at[c])
        for c in range(CHUNKS)
    ]
    east_sources, north_sources, low_sources = load_sources(2, 1, 0), load_sources(3, 1, 1), load_sources(0, 2, 2)
    high_east, low_east = load_maps(2, 2, 1, 0), load_maps(0, 2, 1, 1)
    high_north, low_north = load_maps(2, 3, 1, 2), load_maps(0, 3, 1, 3)
    high_low, low_low = load_maps(2, 0, 2, 4), load_maps(0, 0, 2, 5)
    for copy in load_traces + [high_east] + east_sources + [low_east, high_north] + north_sources + [low_north]:
        copy.start()
    for copy in [high_low] + low_sources + [low_low]:
        copy.start()

    barrier = pltpu.get_barrier_semaphore()
    neighbours = ((has_left, "gx", i - 1), (has_right, "gx", i + 1), (has_below, "gy", j - 1), (has_above, "gy", j + 1))
    for there, axis, index in neighbours:
        @pl.when(there)
        def _():
            pl.semaphore_signal(barrier, inc=1, device_id={axis: index}, device_id_type=MESH)
    pl.semaphore_wait(barrier, sum(there.astype(jnp.int32) for there, _, _ in neighbours))

    def copy_x(t, c, target):
        return pltpu.make_async_remote_copy(
            src_ref=send_x.at[t, c], dst_ref=recv_x.at[t, c], send_sem=ssx.at[t, c], recv_sem=rsx.at[t, c],
            device_id={"gx": target}, device_id_type=MESH,
        )

    def copy_y(t, c, target):
        return pltpu.make_async_remote_copy(
            src_ref=send_y.at[t, c], dst_ref=recv_y.at[t, c], send_sem=ssy.at[t, c], recv_sem=rsy.at[t, c],
            device_id={"gy": target}, device_id_type=MESH,
        )

    def put(copy, there, buffer, t, c, value, target):
        buffer[t, c] = value.astype(buffer.dtype)

        @pl.when(there)
        def _():
            copy(t, c, target).start()

    put_east = functools.partial(put, copy_x, has_right, send_x, target=i + 1)
    put_north = functools.partial(put, copy_y, has_above, send_y, target=j + 1)
    put_west = functools.partial(put, copy_x, has_left, send_x, target=i - 1)
    put_south = functools.partial(put, copy_y, has_below, send_y, target=j - 1)

    def await_y(t, c, there):
        @pl.when(there)
        def _():
            copy_y(t, c, j).wait_recv()

    def await_x(t, c, there):
        @pl.when(there)
        def _():
            copy_x(t, c, i).wait_recv()

    def clear(buffer, there, begin, end):
        @pl.when(jnp.logical_not(there))
        def _():
            buffer[begin:end] = jnp.zeros((end - begin,) + buffer.shape[1:], buffer.dtype)

    def cols(k):
        return slice(k * face, (k + 1) * face)

    for k, put_face, high_copy, low_copy, source_copies in (
        (2, put_east, high_east, low_east, east_sources),
        (3, put_north, high_north, low_north, north_sources),
    ):
        if k == 2:
            for copy in load_traces:
                copy.wait()
        high_copy.wait()
        low_copy.wait()
        for copy in source_copies:
            copy.wait()

        def first(c, carry):
            held_down[c, :, cols(k - 2)] = dot(traces[c, :, high], maps[high, cols(k)]) + sources[c, :, cols(k)]
            put_face(0, c, dot(traces[c, :, low], maps[low, cols(k)]) + held_down[c, :, cols(k - 2)])
            return carry

        lax.fori_loop(0, CHUNKS, first, 0)

    clear(recv_x, has_left, 0, turn)
    clear(recv_y, has_below, 0, turn)
    clear(recv_x, has_right, turn, last)
    clear(recv_y, has_above, turn, last)

    high_low.wait()
    low_low.wait()
    for copy in low_sources:
        copy.wait()

    def from_x(t, c, row, columns):
        return dot(recv_x[t, c], maps[row * face : (row + 1) * face, columns])

    def from_y(t, c, row, columns):
        return dot(recv_y[t, c], maps[(row + 1) * face : (row + 2) * face, columns])

    def down(step, carry, extra=None):
        t, c = step // CHUNKS + 1, step % CHUNKS
        await_y(t - 1, c, has_below)
        partial[...] = from_y(t - 1, c, 0, high) + held_down[c]
        await_x(t - 1, c, has_left)
        put_east(t, c, from_x(t - 1, c, 0, cols(2)) + partial[:, cols(0)])
        put_north(t, c, from_x(t - 1, c, 0, cols(3)) + partial[:, cols(1)])
        if extra is not None:
            extra(c)
        return carry

    def ahead(c):
        first_up[c] = dot(traces[c, :, high], maps[high, low]) + sources[c, :, low]

    lax.fori_loop(0, CHUNKS, functools.partial(down, extra=ahead), 0)
    lax.fori_loop(CHUNKS, (turn - 1) * CHUNKS, down, 0)

    def turned(c, carry):
        await_y(turn - 1, c, has_below)
        partial[...] = from_y(turn - 1, c, 0, low)
        await_x(turn - 1, c, has_left)
        for k, put_face in ((0, put_west), (1, put_south)):
            partial[:, cols(k)] += from_x(turn - 1, c, 0, cols(k))
            put_face(turn, c, partial[:, cols(k)] + first_up[c, :, cols(k)])
        held_up[c] = partial[...] + sources[c, :, low]
        return carry

    lax.fori_loop(0, CHUNKS, turned, 0)

    def late(c):
        held_last[c] = from_x(turn - 1, c, 0, high) + from_y(turn - 1, c, 0, high) + sources[c, :, high]

    def up(step, carry, extra=None):
        t, c = step // CHUNKS + turn + 1, step % CHUNKS
        await_y(t - 1, c, has_above)
        partial[...] = from_y(t - 1, c, 2, low) + held_up[c]
        await_x(t - 1, c, has_right)
        put_west(t, c, from_x(t - 1, c, 2, cols(0)) + partial[:, cols(0)])
        put_south(t, c, from_x(t - 1, c, 2, cols(1)) + partial[:, cols(1)])
        if extra is not None:
            extra(c)
        return carry

    lax.fori_loop(0, CHUNKS, functools.partial(up, extra=late), 0)
    lax.fori_loop(CHUNKS, (last - turn - 1) * CHUNKS, up, 0)

    def store_out(c):
        return pltpu.make_async_copy(result.at[c], out_hbm.at[0, 0, pl.ds(c * rows, rows)], out_sem.at[c])

    for c in range(CHUNKS):
        await_y(last - 1, c, has_above)
        held_up[c] += from_y(last - 1, c, 2, low)
        held_last[c] += from_y(last - 1, c, 2, high)
        await_x(last - 1, c, has_right)
        result[c, :, low] = (from_x(last - 1, c, 2, low) + held_up[c]).astype(result.dtype)
        result[c, :, high] = (from_x(last - 1, c, 2, high) + held_last[c]).astype(result.dtype)
        store_out(c).start()

    def sent(begin, end, there_x, there_y):
        def one(step, carry):
            t, c = step // CHUNKS + begin, step % CHUNKS

            @pl.when(there_x)
            def _():
                copy_x(t, c, i).wait_send()

            @pl.when(there_y)
            def _():
                copy_y(t, c, j).wait_send()

            return carry

        lax.fori_loop(0, (end - begin) * CHUNKS, one, 0)

    sent(0, turn, has_right, has_above)
    sent(turn, last, has_left, has_below)
    for c in range(CHUNKS):
        store_out(c).wait()


def on_device(maps, sources, traces):
    total, width = traces.shape[2:]
    face = width // 4
    rows = total // CHUNKS
    swaps = TICKS - 1

    def faces():
        return pltpu.VMEM((swaps, CHUNKS, rows, face), jnp.bfloat16)

    def wide(columns, dtype):
        return pltpu.VMEM((CHUNKS, rows, columns), dtype)

    dma = pltpu.SemaphoreType.DMA
    return pl.pallas_call(
        sweep,
        out_shape=jax.ShapeDtypeStruct(traces.shape, jnp.bfloat16),
        in_specs=[pl.BlockSpec(memory_space=pl.ANY)] * 3,
        out_specs=pl.BlockSpec(memory_space=pl.ANY),
        scratch_shapes=[
            pltpu.VMEM((width, width), jnp.bfloat16),
            wide(width, jnp.float32),
            wide(width, jnp.bfloat16),
            wide(2 * face, jnp.float32),
            wide(2 * face, jnp.float32),
            wide(2 * face, jnp.float32),
            wide(2 * face, jnp.float32),
            pltpu.VMEM((rows, 2 * face), jnp.float32),
            wide(width, jnp.bfloat16),
            faces(),
            faces(),
            faces(),
            faces(),
            dma((6,)),
            dma((3, CHUNKS)),
            dma((CHUNKS,)),
            dma((CHUNKS,)),
        ]
        + [dma((swaps, CHUNKS))] * 4,
        compiler_params=pltpu.CompilerParams(collective_id=0, has_side_effects=True),
    )(maps, sources, traces)


def solution(mesh):
    spec = P("gx", "gy", None, None)
    return jax.shard_map(on_device, mesh=mesh, in_specs=(spec, spec, spec), out_specs=spec, check_vma=False)
```

```python
import functools

import jax
import jax.numpy as jnp
from jax import lax
from jax.experimental import pallas as pl
from jax.experimental.pallas import tpu as pltpu
from jax.sharding import PartitionSpec as P

TICKS = 8
CHUNKS = 2
MESH = pl.DeviceIdType.MESH


def dot(a, b):
    return jnp.dot(a, b, preferred_element_type=jnp.float32)


def sweep(
    maps_hbm, sources_hbm, traces_hbm, out_hbm,
    maps, sources, traces, held_down, held_up, held_last, first_up, partial, result,
    send_x, send_y, recv_x, recv_y,
    maps_sem, sources_sem, traces_sem, out_sem, ssx, ssy, rsx, rsy,
):
    face = traces.shape[-1] // 4
    rows = traces.shape[1]
    last = TICKS - 1
    turn = TICKS // 2
    low, high = slice(0, 2 * face), slice(2 * face, 4 * face)
    i, j = lax.axis_index("gx"), lax.axis_index("gy")
    px, py = lax.axis_size("gx"), lax.axis_size("gy")
    has_left, has_right = i > 0, i < px - 1
    has_below, has_above = j > 0, j < py - 1

    def load_maps(row, col, col_faces, sem):
        window = (pl.ds(row * face, 2 * face), pl.ds(col * face, col_faces * face))
        return pltpu.make_async_copy(maps_hbm.at[(0, 0) + window], maps.at[window], maps_sem.at[sem])

    def load_sources(col, col_faces, sem):
        columns = pl.ds(col * face, col_faces * face)
        return [
            pltpu.make_async_copy(
                sources_hbm.at[0, 0, pl.ds(c * rows, rows), columns], sources.at[c, :, columns], sources_sem.at[sem, c]
            )
            for c in range(CHUNKS)
        ]

    load_traces = [
        pltpu.make_async_copy(traces_hbm.at[0, 0, pl.ds(c * rows, rows)], traces.at[c], traces_sem.at[c])
        for c in range(CHUNKS)
    ]
    east_sources, north_sources, low_sources = load_sources(2, 1, 0), load_sources(3, 1, 1), load_sources(0, 2, 2)
    high_east, low_east = load_maps(2, 2, 1, 0), load_maps(0, 2, 1, 1)
    high_north, low_north = load_maps(2, 3, 1, 2), load_maps(0, 3, 1, 3)
    high_low, low_low = load_maps(2, 0, 2, 4), load_maps(0, 0, 2, 5)
    for copy in [high_east] + load_traces + east_sources + [low_east, high_north] + north_sources + [low_north]:
        copy.start()

    barrier = pltpu.get_barrier_semaphore()
    neighbours = ((has_left, "gx", i - 1), (has_right, "gx", i + 1), (has_below, "gy", j - 1), (has_above, "gy", j + 1))
    for there, axis, index in neighbours:
        @pl.when(there)
        def _():
            pl.semaphore_signal(barrier, inc=1, device_id={axis: index}, device_id_type=MESH)
    pl.semaphore_wait(barrier, sum(there.astype(jnp.int32) for there, _, _ in neighbours))

    def copy_x(t, c, target):
        return pltpu.make_async_remote_copy(
            src_ref=send_x.at[t, c], dst_ref=recv_x.at[t, c], send_sem=ssx.at[t, c], recv_sem=rsx.at[t, c],
            device_id={"gx": target}, device_id_type=MESH,
        )

    def copy_y(t, c, target):
        return pltpu.make_async_remote_copy(
            src_ref=send_y.at[t, c], dst_ref=recv_y.at[t, c], send_sem=ssy.at[t, c], recv_sem=rsy.at[t, c],
            device_id={"gy": target}, device_id_type=MESH,
        )

    def put(copy, there, buffer, t, c, value, target):
        buffer[t, c] = value.astype(buffer.dtype)

        @pl.when(there)
        def _():
            copy(t, c, target).start()

    put_east = functools.partial(put, copy_x, has_right, send_x, target=i + 1)
    put_north = functools.partial(put, copy_y, has_above, send_y, target=j + 1)
    put_west = functools.partial(put, copy_x, has_left, send_x, target=i - 1)
    put_south = functools.partial(put, copy_y, has_below, send_y, target=j - 1)

    def await_y(t, c, there):
        @pl.when(there)
        def _():
            copy_y(t, c, j).wait_recv()

    def await_x(t, c, there):
        @pl.when(there)
        def _():
            copy_x(t, c, i).wait_recv()

    def clear(buffer, there, begin, end):
        @pl.when(jnp.logical_not(there))
        def _():
            buffer[begin:end] = jnp.zeros((end - begin,) + buffer.shape[1:], buffer.dtype)

    def cols(k):
        return slice(k * face, (k + 1) * face)

    later = [high_low] + low_sources + [low_low]

    for k, put_face, high_copy, low_copy, source_copies in (
        (2, put_east, high_east, low_east, east_sources),
        (3, put_north, high_north, low_north, north_sources),
    ):
        if k == 2:
            for copy in load_traces:
                copy.wait()
        high_copy.wait()
        low_copy.wait()
        for copy in source_copies:
            copy.wait()

        def first(c, carry):
            held_down[c, :, cols(k - 2)] = dot(traces[c, :, high], maps[high, cols(k)]) + sources[c, :, cols(k)]
            put_face(0, c, dot(traces[c, :, low], maps[low, cols(k)]) + held_down[c, :, cols(k - 2)])
            return carry

        lax.fori_loop(0, CHUNKS, first, 0)
        if k == 2:
            for copy in later:
                copy.start()

    clear(recv_x, has_left, 0, turn)
    clear(recv_y, has_below, 0, turn)
    clear(recv_x, has_right, turn, last)
    clear(recv_y, has_above, turn, last)

    high_low.wait()
    low_low.wait()
    for copy in low_sources:
        copy.wait()

    def from_x(t, c, row, columns):
        return dot(recv_x[t, c], maps[row * face : (row + 1) * face, columns])

    def from_y(t, c, row, columns):
        return dot(recv_y[t, c], maps[(row + 1) * face : (row + 2) * face, columns])

    def down(step, carry, extra=None):
        t, c = step // CHUNKS + 1, step % CHUNKS
        await_y(t - 1, c, has_below)
        partial[...] = from_y(t - 1, c, 0, high) + held_down[c]
        await_x(t - 1, c, has_left)
        put_east(t, c, from_x(t - 1, c, 0, cols(2)) + partial[:, cols(0)])
        put_north(t, c, from_x(t - 1, c, 0, cols(3)) + partial[:, cols(1)])
        if extra is not None:
            extra(c)
        return carry

    def ahead(c):
        first_up[c] = dot(traces[c, :, high], maps[high, low]) + sources[c, :, low]

    lax.fori_loop(0, CHUNKS, functools.partial(down, extra=ahead), 0)
    lax.fori_loop(CHUNKS, (turn - 1) * CHUNKS, down, 0)

    def turned(c, carry):
        await_y(turn - 1, c, has_below)
        partial[...] = from_y(turn - 1, c, 0, low)
        await_x(turn - 1, c, has_left)
        for k, put_face in ((0, put_west), (1, put_south)):
            partial[:, cols(k)] += from_x(turn - 1, c, 0, cols(k))
            put_face(turn, c, partial[:, cols(k)] + first_up[c, :, cols(k)])
        held_up[c] = partial[...] + sources[c, :, low]
        return carry

    lax.fori_loop(0, CHUNKS, turned, 0)

    def late(c):
        held_last[c] = from_x(turn - 1, c, 0, high) + from_y(turn - 1, c, 0, high) + sources[c, :, high]

    def up(step, carry, extra=None):
        t, c = step // CHUNKS + turn + 1, step % CHUNKS
        await_y(t - 1, c, has_above)
        partial[...] = from_y(t - 1, c, 2, low) + held_up[c]
        await_x(t - 1, c, has_right)
        put_west(t, c, from_x(t - 1, c, 2, cols(0)) + partial[:, cols(0)])
        put_south(t, c, from_x(t - 1, c, 2, cols(1)) + partial[:, cols(1)])
        if extra is not None:
            extra(c)
        return carry

    lax.fori_loop(0, CHUNKS, functools.partial(up, extra=late), 0)
    lax.fori_loop(CHUNKS, (last - turn - 1) * CHUNKS, up, 0)

    def store_out(c):
        return pltpu.make_async_copy(result.at[c], out_hbm.at[0, 0, pl.ds(c * rows, rows)], out_sem.at[c])

    for c in range(CHUNKS):
        await_y(last - 1, c, has_above)
        held_up[c] += from_y(last - 1, c, 2, low)
        held_last[c] += from_y(last - 1, c, 2, high)
        await_x(last - 1, c, has_right)
        result[c, :, low] = (from_x(last - 1, c, 2, low) + held_up[c]).astype(result.dtype)
        result[c, :, high] = (from_x(last - 1, c, 2, high) + held_last[c]).astype(result.dtype)
        store_out(c).start()

    def sent(begin, end, there_x, there_y):
        def one(step, carry):
            t, c = step // CHUNKS + begin, step % CHUNKS

            @pl.when(there_x)
            def _():
                copy_x(t, c, i).wait_send()

            @pl.when(there_y)
            def _():
                copy_y(t, c, j).wait_send()

            return carry

        lax.fori_loop(0, (end - begin) * CHUNKS, one, 0)

    sent(0, turn, has_right, has_above)
    sent(turn, last, has_left, has_below)
    for c in range(CHUNKS):
        store_out(c).wait()


def on_device(maps, sources, traces):
    total, width = traces.shape[2:]
    face = width // 4
    rows = total // CHUNKS
    swaps = TICKS - 1

    def faces():
        return pltpu.VMEM((swaps, CHUNKS, rows, face), jnp.bfloat16)

    def wide(columns, dtype):
        return pltpu.VMEM((CHUNKS, rows, columns), dtype)

    dma = pltpu.SemaphoreType.DMA
    return pl.pallas_call(
        sweep,
        out_shape=jax.ShapeDtypeStruct(traces.shape, jnp.bfloat16),
        in_specs=[pl.BlockSpec(memory_space=pl.ANY)] * 3,
        out_specs=pl.BlockSpec(memory_space=pl.ANY),
        scratch_shapes=[
            pltpu.VMEM((width, width), jnp.bfloat16),
            wide(width, jnp.float32),
            wide(width, jnp.bfloat16),
            wide(2 * face, jnp.float32),
            wide(2 * face, jnp.float32),
            wide(2 * face, jnp.float32),
            wide(2 * face, jnp.float32),
            pltpu.VMEM((rows, 2 * face), jnp.float32),
            wide(width, jnp.bfloat16),
            faces(),
            faces(),
            faces(),
            faces(),
            dma((6,)),
            dma((3, CHUNKS)),
            dma((CHUNKS,)),
            dma((CHUNKS,)),
        ]
        + [dma((swaps, CHUNKS))] * 4,
        compiler_params=pltpu.CompilerParams(collective_id=0, has_side_effects=True),
    )(maps, sources, traces)


def solution(mesh):
    spec = P("gx", "gy", None, None)
    return jax.shard_map(on_device, mesh=mesh, in_specs=(spec, spec, spec), out_specs=spec, check_vma=False)
```
